32 devices in a mesh: front: 16 (over z, y, x), panel: 2 (over core).
Axes of the slice: x: 2, y: 2, z: 4, core: 2. Of those that a mesh axis runs over, the one named last changes fastest.
Arguments:
- sep_factor: bfloat16 [16384, 1024], P(('front', 'panel')), may hold values from -3 to 3, as said below
- coup_factor: bfloat16 [32768, 1024], P(('front', 'panel')), may hold values from -0.1875 to 0.1875
- coup_list: int32 [16, 16], replicated, may hold values from -1 to 15, as said below
- slot_tiles: int32 [16, 16], replicated, may hold values from 0 to 255, as said below
- anc_tiles: bfloat16 [32768, 128], P('front'), may hold values from -50 to 50
Outputs:
- selected_inverse: float32 [16384, 1024], P(('front', 'panel'))
- variances: float32 [16384], P(('front', 'panel'))
The draws below stay inside these ranges and needn't reach their ends.
Inputs may be any that keep to these rules, and one draw needn't show every extreme that they name: `sep_factor`: each front's block of 1024 rows is lower triangular with a diagonal of 1 or more. `coup_list`: a front's entries name distinct blocks; live entries come first and the rest are -1; every front has 4 or more live entries and some front has 16. `slot_tiles`: every strip id of 0 to 255 appears in exactly one slot; every group holds exactly one strip of each block row.
All inputs are finite; a program needn't handle non-finite values.
Results may differ from the reference program's by a relative error of at most 0.0056.
Values may be sent and summed in bfloat16 or wider, within the bound.
A program may use at most 128 MiB of HBM per device.

```python
import math
import jax
import jax.numpy as jnp
from jax import lax

NS = 1024
BLK = 128
MAXB = 16
NAB = 16
MAXA = 2048
STRIPS = 1
SR = 128
N_FRONT = 16


def slot_layout(key):
    keys = jax.random.split(key, 2)
    strip_count = NAB * N_FRONT
    row_keys = jax.random.split(keys[0], NAB)
    owner = jax.vmap(lambda row_key: jax.random.permutation(row_key, N_FRONT))(row_keys).reshape(-1)
    jitter = jax.random.permutation(keys[1], strip_count)
    order = jnp.argsort(owner * strip_count + jitter, stable=True)
    return order.astype(jnp.int32).reshape(N_FRONT, NAB)


def draw_slot_tiles(key, part):
    return slot_layout(jax.random.fold_in(key, 11))


def draw_anc_tiles(key, part):
    slots = slot_layout(jax.random.fold_in(key, 11)).reshape(-1)
    order_all = NAB * BLK
    noise = jax.random.normal(jax.random.fold_in(key, 12), (order_all, order_all), jnp.float32)
    matrix = (noise + noise.T) * (0.3 / math.sqrt(2.0))
    diagonal = jax.random.uniform(jax.random.fold_in(key, 13), (order_all,), jnp.float32, 1.5, 3.0)
    matrix = matrix + jnp.diag(diagonal)
    matrix = jnp.clip(matrix, -50.0, 50.0)
    strips = matrix.reshape(NAB, STRIPS, SR, NAB, BLK).transpose(0, 3, 1, 2, 4).reshape(NAB * NAB * STRIPS, SR, BLK)
    return strips[slots].reshape(-1, BLK).astype(jnp.bfloat16)


def draw_sep_factor(key, part):
    total_rows = N_FRONT * NS
    noise = jax.random.normal(jax.random.fold_in(key, 21), (total_rows, NS), jnp.float32) * (1.0 / math.sqrt(NS))
    noise = jnp.clip(noise, -1.0, 1.0)
    diagonal = jnp.exp(jax.random.uniform(jax.random.fold_in(key, 22), (total_rows,), jnp.float32, 0.0, math.log(3.0)))
    ratio = jax.random.uniform(jax.random.fold_in(key, 23), (total_rows,), jnp.float32, 0.4, 0.85)
    local_row = jnp.arange(total_rows) % NS
    column = jnp.arange(NS)
    below = local_row[:, None] > column[None, :]
    on_diag = local_row[:, None] == column[None, :]
    next_to = local_row[:, None] == column[None, :] + 1
    result = jnp.where(below & ~next_to, noise, 0.0)
    result = result + jnp.where(on_diag, diagonal[:, None], 0.0)
    result = result + jnp.where(next_to, -(ratio * diagonal)[:, None], 0.0)
    return result.astype(jnp.bfloat16)


def draw_coup_list(key, part):
    keys = jax.random.split(jax.random.fold_in(key, 31), N_FRONT)
    perms = jax.vmap(lambda front_key: jax.random.permutation(front_key, NAB))(keys)[:, :MAXB]
    counts = jax.random.randint(jax.random.fold_in(key, 32), (N_FRONT,), MAXB // 4, MAXB + 1)
    heavy = jax.random.randint(jax.random.fold_in(key, 33), (), 0, N_FRONT)
    counts = jnp.where(jnp.arange(N_FRONT) == heavy, MAXB, counts)
    position = jnp.arange(MAXB)
    return jnp.where(position[None, :] < counts[:, None], perms, -1).astype(jnp.int32)


def level_of(own_key, extent, cuts, low, largest):
    factor_of = 1.0
    for dim, parts in cuts:
        heights = jax.random.uniform(jax.random.fold_in(jax.random.fold_in(own_key, 6), dim), (parts,), jnp.float32, low / len(cuts), largest / len(cuts))
        factor_of = factor_of * jnp.repeat(jnp.exp(heights), extent[dim] // parts).reshape((-1,) + (1,) * (len(extent) - 1 - dim))
    return factor_of


def normal_values(stream_key, dims, spread, reach, shards=(), held_as=jnp.bfloat16):
    values = jax.random.normal(stream_key, dims, jnp.float32) * spread
    if len(shards) > 0:
        values = level_of(stream_key, dims, shards, -0.22, 0.18) * values
    return jnp.clip(values, min=-reach, max=reach).astype(held_as)


def setup_inputs(seed: int = 0) -> dict:
    key_of = jax.random.split(jax.random.key(seed), 6)
    return {
        "sep_factor": draw_sep_factor(jax.random.fold_in(key_of[5], 71), 0),
        "coup_factor": normal_values(key_of[1], (N_FRONT * MAXA, NS), NS ** -0.5, 0.1875, ((0, 32),)),
        "coup_list": draw_coup_list(jax.random.fold_in(key_of[5], 71), 0),
        "slot_tiles": draw_slot_tiles(jax.random.fold_in(key_of[5], 71), 0),
        "anc_tiles": draw_anc_tiles(jax.random.fold_in(key_of[5], 71), 0),
    }


def reference(sep_factor, coup_factor, coup_list, slot_tiles, anc_tiles):
    pool_strips = jnp.zeros((NAB * NAB * STRIPS, SR, BLK), anc_tiles.dtype)
    pool_strips = pool_strips.at[slot_tiles.reshape(-1)].set(anc_tiles.reshape(-1, SR, BLK))
    pool_tiles = pool_strips.reshape(NAB, NAB, BLK, BLK)
    identity = jnp.eye(NS, dtype=jnp.float32)

    def per_front(front_index):
        lower_full = lax.dynamic_slice_in_dim(sep_factor, front_index * NS, NS, 0).astype(jnp.float32)
        inverse = lax.linalg.triangular_solve(lower_full, identity, left_side=True, lower=True)
        coupling = lax.dynamic_slice_in_dim(coup_factor, front_index * MAXA, MAXA, 0)
        blocks = coup_list[front_index]
        live_blocks = blocks >= 0
        safe_blocks = jnp.where(live_blocks, blocks, 0)
        row_live = jnp.repeat(live_blocks, BLK)
        coupling = jnp.where(row_live[:, None], coupling, jnp.zeros_like(coupling))
        wide_full = jnp.dot(coupling.astype(jnp.float32), inverse.astype(jnp.bfloat16).astype(jnp.float32), preferred_element_type=jnp.float32).astype(jnp.bfloat16)
        picked = pool_tiles[safe_blocks][:, safe_blocks]
        both_live = live_blocks[:, None] & live_blocks[None, :]
        picked = jnp.where(both_live[:, :, None, None], picked, jnp.zeros_like(picked))
        sigma_pair = picked.transpose(0, 2, 1, 3).reshape(MAXA, MAXA)
        carried = jnp.dot(sigma_pair.astype(jnp.float32), wide_full.astype(jnp.float32), preferred_element_type=jnp.float32).astype(jnp.bfloat16)
        product = jnp.dot(wide_full.T.astype(jnp.float32), carried.astype(jnp.float32), preferred_element_type=jnp.float32)
        inverse_square = jnp.dot(inverse.T, inverse, precision=lax.Precision.HIGHEST)
        selected = inverse_square + product
        return (selected, jnp.diagonal(selected))
    selected_all, variances = lax.map(per_front, jnp.arange(N_FRONT, dtype=jnp.int32))
    return (selected_all.reshape(N_FRONT * NS, NS), variances.reshape(N_FRONT * NS))
```

```python
import functools

import jax
import jax.numpy as jnp
from jax import lax
from jax.experimental import pallas as pl
from jax.experimental.pallas import tpu as pltpu
from jax.sharding import PartitionSpec as P

BF = jnp.bfloat16
F32 = jnp.float32
DIAG = 128
MESH = pl.DeviceIdType.MESH


def mm(a, b):
    return jnp.dot(a, b, preferred_element_type=F32)


def split(x):
    hi = x.astype(BF)
    return hi, (x - hi.astype(F32)).astype(BF)


def flip(index, mask):
    bit = 1
    while bit <= mask:
        if mask & bit:
            index = index + bit * (1 - 2 * ((index // bit) % 2))
        bit *= 2
    return index


def first_kernel(
    depth,
    sep_ref,
    coup_ref,
    anc_ref,
    wide_out,
    wide_other,
    square_out,
    pool_ref,
    inv_ref,
    wide_ref,
    square_ref,
    lmat,
    coup_all,
    xl,
    xd,
    panel_send,
    panel_recv,
    z_recv,
    x_recv,
    y_recv,
    first_recv,
    second_recv,
    share_recv,
    out_send,
    local_sem,
):
    me = lax.axis_index("panel")
    group = lax.axis_index("front")
    layer, spot = group // 4, group % 4
    half, n = sep_ref.shape[0], sep_ref.shape[1]
    slab = anc_ref.shape[0]
    part = slab // 2
    partner = (group, 1 - me)
    beside = (layer * 4 + flip(spot, 1), me)
    behind = (layer * 4 + flip(spot, 2), me)
    peers = [(flip(layer, k) * 4 + spot, me) for k in range(1, depth)]

    barrier = pltpu.get_barrier_semaphore()
    for device in [partner, beside, behind] + peers:
        pl.semaphore_signal(barrier, inc=1, device_id=device, device_id_type=MESH)
    pl.semaphore_wait(barrier, 2 + depth)

    def remote(source, target, send, recv, device):
        return pltpu.make_async_remote_copy(
            src_ref=source, dst_ref=target, send_sem=send, recv_sem=recv, device_id=device, device_id_type=MESH
        )

    def place(k, mask, low=0, size=part):
        owner = flip(layer, k) * 4 + flip(spot, mask)
        start = pl.multiple_of(owner * slab + me * part + low, part // 2)
        return pool_ref.at[pl.ds(start, size), :]

    def push(source, target, recv, device):
        remote(source, target, out_send, recv, device).start()

    def arrived(target, recv):
        remote(target, target, out_send, recv, partner).wait_recv()

    own = anc_ref.at[pl.ds(pl.multiple_of(me * part, part), part), :]

    def open_block(k):
        source = own if k == 0 else place(k, 0)
        if k > 0:
            arrived(source, z_recv.at[k])
        piece = part // 2
        for first in (True, False):
            for recv, device, low in (
                (x_recv, beside, piece if first else 0),
                (y_recv, behind, 0 if first else piece),
            ):
                push(
                    source.at[pl.ds(low, piece), :],
                    place(k, 0, low, piece),
                    recv.at[k if first else depth + k],
                    device,
                )
        if k > 0:
            push(source, source, share_recv, partner)

    def relay(k):
        piece = part // 2
        arrived(place(k, 1, piece, piece), x_recv.at[k])
        push(place(k, 1, piece, piece), place(k, 1, piece, piece), second_recv.at[k], behind)
        arrived(place(k, 2, 0, piece), y_recv.at[k])
        push(place(k, 2, 0, piece), place(k, 2, 0, piece), first_recv.at[k], beside)
        arrived(place(k, 1, 0, piece), x_recv.at[depth + k])
        arrived(place(k, 2, piece, piece), y_recv.at[depth + k])
        push(place(k, 1), place(k, 1), share_recv, partner)
        push(place(k, 2), place(k, 2), share_recv, partner)

    def finish(k):
        piece = part // 2
        arrived(place(k, 3, 0, piece), first_recv.at[k])
        arrived(place(k, 3, piece, piece), second_recv.at[k])
        push(place(k, 3), place(k, 3), share_recv, partner)

    def stage(k):
        if 2 <= k <= depth + 1:
            finish(k - 2)
        if 1 <= k <= depth:
            relay(k - 1)
        if k < depth:
            open_block(k)

    rows = coup_ref.shape[0]
    upper = pl.ds(pl.multiple_of(me * half, half), half)
    sep_copy = remote(sep_ref, lmat.at[upper, :], panel_send.at[0], panel_recv.at[0], partner)
    coup_copy = remote(coup_ref, coup_all.at[pl.ds(rows, rows), :], panel_send.at[1], panel_recv.at[1], partner)
    wide_copy = remote(wide_ref, wide_other, panel_send.at[2], panel_recv.at[2], partner)
    sep_keep = pltpu.make_async_copy(sep_ref, lmat.at[upper, :], local_sem.at[0])
    sep_copy.start()
    for k in range(1, depth):
        push(own, place(0, 0), z_recv.at[k], peers[k - 1])
        if k == 1:
            stage(0)
    coup_copy.start()
    sep_keep.start()
    coup_keep = pltpu.make_async_copy(coup_ref, coup_all.at[pl.ds(0, rows), :], local_sem.at[1])
    coup_keep.start()
    keep = pltpu.make_async_copy(
        anc_ref, pool_ref.at[pl.ds(pl.multiple_of(group * slab, slab), slab), :], local_sem.at[2]
    )
    keep.start()

    inv_ref[...] = jnp.zeros_like(inv_ref)
    xl[...] = jnp.zeros_like(xl)
    sep_keep.wait()
    remote(sep_ref, lmat.at[pl.ds(pl.multiple_of((1 - me) * half, half), half), :], panel_send.at[0], panel_recv.at[0], partner).wait_recv()

    blocks = n // DIAG
    row = lax.broadcasted_iota(jnp.int32, (DIAG, DIAG), 0)
    col = lax.broadcasted_iota(jnp.int32, (DIAG, DIAG), 1)
    eye = row == col
    for b in range(blocks):
        span = pl.ds(b * DIAG, DIAG)
        block = lmat[span, span].astype(F32)
        xd[b] = jnp.where(eye, 1.0 / jnp.where(eye, block, 1.0), 0.0)

    def level(step, carry):
        mask = (
            ((row >> (step + 1)) == (col >> (step + 1)))
            & (((row >> step) & 1) == 1)
            & (((col >> step) & 1) == 0)
        )
        for b in range(blocks):
            span = pl.ds(b * DIAG, DIAG)
            x = xd[b]
            hi, lo = split(x)
            below = jnp.where(mask, lmat[span, span].astype(F32), 0.0).astype(BF)
            y = mm(below, jnp.concatenate([hi, lo], axis=1))
            yhi, ylo = split(y[:, :DIAG] + y[:, DIAG:])
            t = mm(jnp.concatenate([hi, lo], axis=0), jnp.concatenate([yhi, ylo], axis=1))
            t = (t[:DIAG, :DIAG] + t[:DIAG, DIAG:]) + (t[DIAG:, :DIAG] + t[DIAG:, DIAG:])
            xd[b] = x - t
        return carry

    levels = DIAG.bit_length() - 1
    lax.fori_loop(0, levels // 2, level, 0)
    stage(1)
    lax.fori_loop(levels // 2, levels, level, 0)
    for b in range(blocks):
        span = pl.ds(b * DIAG, DIAG)
        inv_ref[span, span], xl[span, span] = split(xd[b])
    size = DIAG
    while size < n:
        for start in range(0, n, 2 * size):
            top, low = pl.ds(start, size), pl.ds(start + size, size)
            below = lmat[low, top]
            thi, tlo = split(mm(below, inv_ref[top, top]) + mm(below, xl[top, top]))
            t = mm(inv_ref[low, low], thi) + (mm(inv_ref[low, low], tlo) + mm(xl[low, low], thi))
            inv_ref[low, top], xl[low, top] = split(-t)
        size *= 2
    stage(2)

    chunk = min(512, rows)
    columns = pl.ds(pl.multiple_of(me * half, half), half)
    coup_keep.wait()
    coup_copy.wait_recv()

    @pl.loop(0, 2 * rows // chunk)
    def _(i):
        take = pl.ds(pl.multiple_of(i * chunk, chunk), chunk)
        wide_ref[take, :] = mm(coup_all[take, :], inv_ref[:, columns]).astype(BF)

    stage(3)
    wide_copy.start()
    wide_keep = pltpu.make_async_copy(wide_ref, wide_out, local_sem.at[3])
    wide_keep.start()
    strip = pool_ref.shape[0] - 4 * depth * slab
    blank = pltpu.make_async_copy(
        inv_ref.at[pl.ds(0, strip), pl.ds(n - DIAG, DIAG)], pool_ref.at[pl.ds(4 * depth * slab, strip), :], local_sem.at[4]
    )
    blank.start()

    @pl.loop(0, n // 256)
    def _(i):
        take = pl.ds(pl.multiple_of(i * 256, 256), 256)
        square_ref[:, take] = lax.dot_general(
            inv_ref[:, columns], inv_ref[:, take], (((0,), (0,)), ((), ())), preferred_element_type=F32
        )

    square_keep = pltpu.make_async_copy(square_ref, square_out, local_sem.at[5])
    square_keep.start()
    for k in range(4, depth + 2):
        stage(k)

    total = 4 * depth - 1
    shared = pool_ref.at[pl.ds(0, total * part), :]
    remote(shared, shared, out_send, share_recv, partner).wait_recv()
    sent = pool_ref.at[pl.ds(0, (2 * total) * part), :]
    remote(sent, sent, out_send, share_recv, partner).wait_send()
    for copy in (keep, wide_keep, blank, square_keep):
        copy.wait()
    sep_copy.wait_send()
    coup_copy.wait_send()
    wide_copy.wait()


def last_kernel(
    list_ref,
    slot_ref,
    wide_in,
    other_in,
    square_in,
    pool_ref,
    out_ref,
    var_ref,
    sigma,
    wide,
    wide_other,
    carried,
    out,
    place,
    tile_sem,
    load_sem,
    store_sem,
):
    me = lax.axis_index("panel")
    group = lax.axis_index("front")
    rows, half = wide.shape
    edge = pool_ref.shape[1]
    groups, slots = slot_ref.shape
    total = groups * slots
    strip_rows = rows * rows // (total * edge)
    strip_count = edge // strip_rows
    across = rows // edge
    chunks = tile_sem.shape[0]
    chunk = rows // chunks
    low, high = pl.ds(0, rows // 2), pl.ds(rows // 2, rows // 2)

    load_wide = pltpu.make_async_copy(wide_in, wide, load_sem.at[0])
    load_low = pltpu.make_async_copy(other_in.at[high, :], wide_other.at[low, :], load_sem.at[1])
    load_high = pltpu.make_async_copy(other_in.at[low, :], wide_other.at[high, :], load_sem.at[2])
    load_square = pltpu.make_async_copy(square_in, out, load_sem.at[3])
    load_wide.start()

    @pl.loop(0, groups)
    def _(g):
        for s in range(slots):
            place[slot_ref[g, s]] = g * slots + s

    def block(i):
        return list_ref[group, (i + me * (across // 2)) % across]

    def fetch(i):
        a = block(i)
        for j in range(across):
            b = block(j)
            live = (a >= 0) & (b >= 0)
            for q in range(strip_count):
                at = place[jnp.where(live, a * groups + b * strip_count + q, 0)]
                source = pl.multiple_of(jnp.where(live, at, total) * strip_rows, strip_rows)
                down = pl.multiple_of(i * edge + q * strip_rows, strip_rows)
                pltpu.make_async_copy(
                    pool_ref.at[pl.ds(source, strip_rows), :],
                    sigma.at[pl.ds(down, strip_rows), pl.ds(j * edge, edge)],
                    tile_sem.at[i // (across // chunks)],
                ).start()

    pl.loop(0, across)(fetch)
    load_low.start()
    load_high.start()
    load_square.start()
    load_wide.wait()

    @pl.loop(0, chunks)
    def _(i):
        take = pl.ds(pl.multiple_of(i * chunk, chunk), chunk)
        pltpu.make_async_copy(sigma.at[take, :], sigma.at[take, :], tile_sem.at[i]).wait()
        carried[:, take] = mm(sigma[take, :], wide[...]).T.astype(BF)

    load_low.wait()
    load_high.wait()
    load_square.wait()
    step = 256
    for source, base in ((wide, me), (wide_other, 1 - me)):
        for c in range(half // step):
            put = pl.ds(pl.multiple_of(base * half + c * step, step), step)
            out[:, put] += mm(carried[...], source[:, pl.ds(c * step, step)])
            pltpu.make_async_copy(out.at[:, put], out_ref.at[:, put], store_sem).start()
    block_out = out[:, pl.ds(pl.multiple_of(me * half, half), half)]
    row = lax.broadcasted_iota(jnp.int32, (half, half), 0)
    col = lax.broadcasted_iota(jnp.int32, (half, half), 1)
    var_ref[...] = jnp.sum(jnp.where(row == col, block_out, 0.0), axis=0, keepdims=True)
    pltpu.make_async_copy(out, out_ref, store_sem).wait()


def gather_kernel(
    depth,
    slot_ref,
    sep_ref,
    coup_ref,
    anc_ref,
    pool,
    wide,
    turned,
    out,
    strips,
    lmat,
    coup,
    inv_ref,
    xl,
    xd,
    panel_send,
    panel_recv,
    z_recv,
    x_recv,
    y_recv,
    first_recv,
    second_recv,
    share_recv,
    out_send,
    local_sem,
):
    me = lax.axis_index("panel")
    group = lax.axis_index("front")
    layer, spot = group // 4, group % 4
    half, n = sep_ref.shape
    groups, slots = slot_ref.shape
    edge = anc_ref.shape[1]
    side = edge // 2
    rows = coup_ref.shape[0]
    across = 2 * rows // edge
    mine = slots // 2
    body = mine * side
    part = body + across
    low_size = part // 32 * 16
    low_size = part - low_size if part % 32 else low_size
    partner = (group, 1 - me)
    beside = (layer * 4 + flip(spot, 1), me)
    behind = (layer * 4 + flip(spot, 2), me)
    peers = [(flip(layer, k) * 4 + spot, me) for k in range(1, depth)]

    strip_load = pltpu.make_async_copy(
        anc_ref.at[pl.ds(pl.multiple_of(me * mine * edge, mine * edge), mine * edge), :], strips, local_sem.at[0]
    )
    strip_load.start()
    upper = pl.ds(pl.multiple_of(me * half, half), half)
    sep_keep = pltpu.make_async_copy(sep_ref, lmat.at[upper, :], local_sem.at[1])
    sep_keep.start()
    coup_keep = pltpu.make_async_copy(coup_ref, coup, local_sem.at[2])
    coup_keep.start()

    barrier = pltpu.get_barrier_semaphore()
    for device in [partner, beside, behind] + peers:
        pl.semaphore_signal(barrier, inc=1, device_id=device, device_id_type=MESH)

    def remote(source, target, send, recv, device):
        return pltpu.make_async_remote_copy(
            src_ref=source, dst_ref=target, send_sem=send, recv_sem=recv, device_id=device, device_id_type=MESH
        )

    def place(k, mask, piece=None):
        owner = flip(layer, k) * 4 + flip(spot, mask)
        low, size = ((0, part), (0, low_size), (low_size, part - low_size))[0 if piece is None else piece + 1]
        start = pl.multiple_of((owner * 2 + me) * part + low, 16)
        return pool.at[pl.ds(start, size), :]

    def push(source, recv, device):
        remote(source, source, out_send, recv, device).start()

    def arrived(target, recv):
        remote(target, target, out_send, recv, partner).wait_recv()

    def open_block(k):
        if k > 0:
            arrived(place(k, 0), z_recv.at[k])
        for first in (True, False):
            for recv, device, piece in ((x_recv, beside, 1 if first else 0), (y_recv, behind, 0 if first else 1)):
                push(place(k, 0, piece), recv.at[k if first else depth + k], device)
        push(place(k, 0), share_recv, partner)

    def relay(k):
        arrived(place(k, 1, 1), x_recv.at[k])
        push(place(k, 1, 1), second_recv.at[k], behind)
        arrived(place(k, 2, 0), y_recv.at[k])
        push(place(k, 2, 0), first_recv.at[k], beside)

    def collect(k):
        arrived(place(k, 1, 0), x_recv.at[depth + k])
        arrived(place(k, 2, 1), y_recv.at[depth + k])
        push(place(k, 1), share_recv, partner)
        push(place(k, 2), share_recv, partner)

    def finish(k):
        arrived(place(k, 3, 0), first_recv.at[k])
        arrived(place(k, 3, 1), second_recv.at[k])
        push(place(k, 3), share_recv, partner)

    row = lax.broadcasted_iota(jnp.int32, (side, edge), 0)
    lane = lax.broadcasted_iota(jnp.int32, (side, edge), 1)
    left = lane < side
    column = jnp.where(left, lane, lane - side)
    left_flag = jnp.where(left, 1, 0)
    triangle = jnp.where(column >= row, 1, 0)
    list_row = lax.broadcasted_iota(jnp.int32, (across, edge), 0)
    mine_at = pl.multiple_of((group * 2 + me) * part, 16)
    strip_load.wait()
    extra = jnp.zeros((across, edge), F32)
    for s in range(mine):
        tile_id = slot_ref[group, me * mine + s]
        i, j = tile_id // across, tile_id % across
        tile = strips[s * edge : (s + 1) * edge, :].astype(F32)
        chosen = jnp.where(jnp.full((edge, edge), i - j) > 0, tile.T, tile)
        top, bottom = chosen[:side, :], chosen[side:, :]
        gap = jnp.full((side, edge), i - j)
        wanted = jnp.where(gap == 0, triangle, jnp.where(gap < 0, 1, 0))
        pool[pl.ds(mine_at + s * side, side), :] = jnp.where(left_flag == wanted, top, bottom).astype(BF)
        line = jnp.sum(jnp.where(column == row, jnp.where(left, bottom, top), 0.0), axis=0, keepdims=True)
        hit = jnp.where(jnp.full((across, edge), i - j) == 0, jnp.where(list_row == jnp.full((across, edge), i), 1, 0), 0)
        extra = extra + jnp.where(hit == 1, line, 0.0)
    pool[pl.ds(mine_at + body, across), :] = extra.astype(BF)

    pl.semaphore_wait(barrier, 2 + depth)
    sep_copy = remote(sep_ref, lmat.at[upper, :], panel_send.at[0], panel_recv.at[0], partner)
    sep_copy.start()
    for k in range(1, depth):
        push(place(0, 0), z_recv.at[k], peers[k - 1])
        if k == 1:
            open_block(0)

    inv_ref[...] = jnp.zeros_like(inv_ref)
    xl[...] = jnp.zeros_like(xl)
    wide[pl.ds(2 * rows, edge), :] = jnp.zeros((edge, n), BF)
    turned[:, pl.ds(2 * rows, edge)] = jnp.zeros((half, edge), BF)
    sep_keep.wait()
    other = pl.ds(pl.multiple_of((1 - me) * half, half), half)
    remote(sep_ref, lmat.at[other, :], panel_send.at[0], panel_recv.at[0], partner).wait_recv()

    blocks = n // DIAG
    row128 = lax.broadcasted_iota(jnp.int32, (DIAG, DIAG), 0)
    col128 = lax.broadcasted_iota(jnp.int32, (DIAG, DIAG), 1)
    eye = row128 == col128
    for b in range(blocks):
        span = pl.ds(b * DIAG, DIAG)
        block = lmat[span, span].astype(F32)
        xd[b] = jnp.where(eye, 1.0 / jnp.where(eye, block, 1.0), 0.0)

    def level(step, carry):
        mask = (
            ((row128 >> (step + 1)) == (col128 >> (step + 1)))
            & (((row128 >> step) & 1) == 1)
            & (((col128 >> step) & 1) == 0)
        )
        for b in range(blocks):
            span = pl.ds(b * DIAG, DIAG)
            x = xd[b]
            hi, lo = split(x)
            below = jnp.where(mask, lmat[span, span].astype(F32), 0.0).astype(BF)
            y = mm(below, jnp.concatenate([hi, lo], axis=1))
            yhi, ylo = split(y[:, :DIAG] + y[:, DIAG:])
            t = mm(jnp.concatenate([hi, lo], axis=0), jnp.concatenate([yhi, ylo], axis=1))
            t = (t[:DIAG, :DIAG] + t[:DIAG, DIAG:]) + (t[DIAG:, :DIAG] + t[DIAG:, DIAG:])
            xd[b] = x - t
        return carry

    def merge(size):
        for start in range(0, n, 2 * size):
            top, low = pl.ds(start, size), pl.ds(start + size, size)
            below = lmat[low, top]
            thi, tlo = split(mm(below, inv_ref[top, top]) + mm(below, xl[top, top]))
            t = mm(inv_ref[low, low], thi) + (mm(inv_ref[low, low], tlo) + mm(xl[low, low], thi))
            inv_ref[low, top], xl[low, top] = split(-t)

    levels = DIAG.bit_length() - 1
    lax.fori_loop(0, levels // 2, level, 0)
    relay(0)
    open_block(1)
    collect(0)
    lax.fori_loop(levels // 2, levels, level, 0)
    for b in range(blocks):
        span = pl.ds(b * DIAG, DIAG)
        inv_ref[span, span], xl[span, span] = split(xd[b])
    relay(1)
    merge(DIAG)
    open_block(2)
    finish(0)
    collect(1)
    size = 2 * DIAG
    while size < n:
        merge(size)
        size *= 2
    relay(2)
    coup_keep.wait()
    own_rows = pl.ds(pl.multiple_of(me * rows, rows), rows)
    step = 256
    for c in range(n // step):
        put = pl.ds(c * step, step)
        deep = pl.ds(c * step, n - c * step)
        wide[own_rows, put] = mm(coup[:, deep], inv_ref[deep, put]).astype(BF)
    open_block(3)
    finish(1)
    collect(2)
    wide_copy = remote(wide.at[own_rows, :], wide.at[own_rows, :], panel_send.at[1], panel_recv.at[1], partner)
    wide_copy.start()
    columns = pl.ds(pl.multiple_of(me * half, half), half)

    @pl.loop(0, n // step)
    def _(i):
        take = pl.ds(pl.multiple_of(i * step, step), step)
        out[:, take] = lax.dot_general(
            inv_ref[:, columns], inv_ref[:, take], (((0,), (0,)), ((), ())), preferred_element_type=F32
        )

    relay(3)
    finish(2)
    other_rows = pl.ds(pl.multiple_of((1 - me) * rows, rows), rows)
    remote(wide.at[other_rows, :], wide.at[other_rows, :], panel_send.at[1], panel_recv.at[1], partner).wait_recv()

    @pl.loop(0, across)
    def _(c):
        put = pl.ds(pl.multiple_of(c * edge, edge), edge)
        turned[:, put] = wide[put, columns].T

    collect(3)
    finish(3)
    total = 4 * depth
    shared = pool.at[pl.ds(0, total * part), :]
    remote(shared, shared, out_send, share_recv, partner).wait_recv()

    sent = pool.at[pl.ds(0, (2 * total - 1) * part), :]
    remote(sent, sent, out_send, share_recv, partner).wait_send()
    sep_copy.wait_send()
    wide_copy.wait_send()


def select_kernel(
    list_ref,
    slot_ref,
    pool,
    wide,
    flat,
    square,
    out_ref,
    var_ref,
    table,
    natural,
    turned,
    sigma,
    carried,
    out,
    load_sem,
    store_sem,
):
    me = lax.axis_index("panel")
    group = lax.axis_index("front")
    groups, slots = slot_ref.shape
    edge = pool.shape[1]
    side = edge // 2
    half, n = out.shape
    across = sigma.shape[0] // edge
    rows = sigma.shape[0] // 2
    mine = slots // 2
    body = mine * side
    part = body + across
    step = 256
    columns = pl.ds(pl.multiple_of(me * half, half), half)

    for c in range(across):
        at = across
        for a in range(across):
            at = jnp.where(list_ref[group, a] == c, a, at)
        source = pl.ds(pl.multiple_of(at * edge, edge), edge)
        put = pl.ds(c * edge, edge)
        pltpu.make_async_copy(flat.at[:, source], turned.at[:, put], load_sem.at[0]).start()
        pltpu.make_async_copy(wide.at[source, :], natural.at[put, :], load_sem.at[1]).start()

    @pl.loop(0, groups)
    def _(g):
        for s in range(slots):
            table[slot_ref[g, s]] = (g * 2 + s // mine) * part + (s % mine) * side

    row = lax.broadcasted_iota(jnp.int32, (side, edge), 0)
    lane = lax.broadcasted_iota(jnp.int32, (side, edge), 1)
    left = lane < side
    column = jnp.where(left, lane, lane - side)

    def packed(i, j):
        tile_id = i * across + j
        return pool[pl.ds(pl.multiple_of(table[tile_id], 16), side), :]

    def span_of(i):
        return pl.ds(pl.multiple_of(i * edge, edge), edge)

    extra = jnp.zeros((across, edge), F32)
    for g in range(2 * groups):
        extra = extra + pool[g * part + body : g * part + part, :].astype(F32)

    for i in range(across):
        p = packed(i, i).astype(F32)
        turn = jnp.concatenate([p, p], axis=0).T
        d = jnp.broadcast_to(extra[i : i + 1, :], (side, edge))
        keep, below, equal = column >= row, column < row, column == row
        top = jnp.where(left, jnp.where(keep, p, turn[:side]), jnp.where(below, p, jnp.where(equal, d, turn[:side])))
        bottom = jnp.where(left, jnp.where(below, p, jnp.where(equal, d, turn[side:])), jnp.where(keep, p, turn[side:]))
        sigma[i * edge : (i + 1) * edge, i * edge : (i + 1) * edge] = jnp.concatenate([top, bottom], axis=0).astype(BF)

    @pl.loop(0, across)
    def _(i):
        for d in range(1, across // 2 + 1):
            other = (i + d) % across
            a, b = jnp.minimum(i, other), jnp.maximum(i, other)
            p, q = packed(a, b), packed(b, a)
            sigma[span_of(a), span_of(b)] = jnp.concatenate([jnp.where(left, p, q), jnp.where(left, q, p)], axis=0)

    for i in range(0, across, 2):
        a, b = slice(i * edge, (i + 1) * edge), slice((i + 1) * edge, (i + 2) * edge)
        sigma[b, a] = sigma[a, b].astype(F32).T.astype(BF)

    pltpu.make_async_copy(turned, turned, load_sem.at[0]).wait()
    size = 2 * rows
    for c in range(size // step):
        put = slice(c * step, (c + 1) * step)
        end = (c + 1) * step
        value = mm(turned[:, :end], sigma[:end, put])
        if end < size:
            value = value + lax.dot_general(
                turned[:, end:], sigma[put, end:], (((1,), (1,)), ((), ())), preferred_element_type=F32
            )
        carried[:, put] = value.astype(BF)

    pltpu.make_async_copy(natural, natural, load_sem.at[1]).wait()
    for c in range(n // step):
        put = slice(c * step, (c + 1) * step)
        out[:, put] = square[:, put] + mm(carried[...], natural[:, put])
        pltpu.make_async_copy(out.at[:, put], out_ref.at[:, put], store_sem).start()
    block_out = out[:, columns]
    row_out = lax.broadcasted_iota(jnp.int32, (half, half), 0)
    col_out = lax.broadcasted_iota(jnp.int32, (half, half), 1)
    var_ref[...] = jnp.sum(jnp.where(row_out == col_out, block_out, 0.0), axis=0, keepdims=True)
    pltpu.make_async_copy(out, out_ref, store_sem).wait()


def on_device(sep_factor, coup_factor, coup_list, slot_tiles, anc_tiles):
    panels = lax.axis_size("panel")
    groups = lax.axis_size("front")
    half, width = sep_factor.shape
    edge = anc_tiles.shape[1]
    slots = slot_tiles.shape[1]
    strip_rows = anc_tiles.shape[0] // slots
    rows = coup_list.shape[1] * edge
    vmem = pl.BlockSpec(memory_space=pltpu.VMEM)
    smem = pl.BlockSpec(memory_space=pltpu.SMEM)
    hbm = pl.BlockSpec(memory_space=pltpu.HBM)
    depth = groups // 4
    dma = pltpu.SemaphoreType.DMA
    if strip_rows == edge:
        part = slots // 2 * (edge // 2) + rows // edge
        pool, wide, turned, square = pl.pallas_call(
            functools.partial(gather_kernel, depth),
            out_shape=(
                pltpu.VMEM((2 * groups * part, edge), BF),
                pltpu.VMEM((rows + edge, width), BF),
                pltpu.VMEM((half, rows + edge), BF),
                pltpu.VMEM((half, width), F32),
            ),
            in_specs=[smem] + [hbm] * 3,
            out_specs=[vmem] * 4,
            scratch_shapes=[
                pltpu.VMEM((slots // 2 * edge, edge), BF),
                pltpu.VMEM((width, width), BF),
                pltpu.VMEM((rows // 2, width), BF),
                pltpu.VMEM((width, width), BF),
                pltpu.VMEM((width, width), BF),
                pltpu.VMEM((width // DIAG, DIAG, DIAG), F32),
                dma((2,)),
                dma((2,)),
                dma((depth,)),
                dma((2 * depth,)),
                dma((2 * depth,)),
                dma((depth,)),
                dma((depth,)),
                dma,
                dma,
                dma((3,)),
            ],
            compiler_params=pltpu.CompilerParams(
                vmem_limit_bytes=50 << 20, collective_id=0, has_side_effects=True
            ),
        )(slot_tiles, sep_factor, coup_factor, anc_tiles)
        selected, variances = pl.pallas_call(
            select_kernel,
            out_shape=(
                jax.ShapeDtypeStruct((half, width), F32),
                jax.ShapeDtypeStruct((1, half), F32),
            ),
            in_specs=[smem, smem] + [vmem] * 4,
            out_specs=[hbm, vmem],
            scratch_shapes=[
                pltpu.SMEM((groups * slots,), jnp.int32),
                pltpu.VMEM((rows, width), BF),
                pltpu.VMEM((half, rows), BF),
                pltpu.VMEM((rows, rows), BF),
                pltpu.VMEM((half, rows), BF),
                pltpu.VMEM((half, width), F32),
                dma((2,)),
                dma,
            ],
            compiler_params=pltpu.CompilerParams(vmem_limit_bytes=50 << 20),
        )(coup_list, slot_tiles, pool, wide, turned, square)
        return selected, variances.reshape(half)
    wide, wide_other, square, pool = pl.pallas_call(
        functools.partial(first_kernel, depth),
        out_shape=(
            jax.ShapeDtypeStruct((rows, half), BF),
            jax.ShapeDtypeStruct((rows, half), BF),
            jax.ShapeDtypeStruct((half, width), F32),
            jax.ShapeDtypeStruct((groups * anc_tiles.shape[0] + strip_rows, edge), BF),
        ),
        in_specs=[hbm] * 3,
        out_specs=[hbm] * 4,
        scratch_shapes=[
            pltpu.VMEM((width, width), BF),
            pltpu.VMEM((rows, half), BF),
            pltpu.VMEM((half, width), F32),
            pltpu.VMEM((width, width), BF),
            pltpu.VMEM((rows, width), BF),
            pltpu.VMEM((width, width), BF),
            pltpu.VMEM((width // DIAG, DIAG, DIAG), F32),
            dma((3,)),
            dma((3,)),
            dma((depth,)),
            dma((2 * depth,)),
            dma((2 * depth,)),
            dma((depth,)),
            dma((depth,)),
            dma,
            dma,
            dma((6,)),
        ],
        compiler_params=pltpu.CompilerParams(
            vmem_limit_bytes=63 << 20, collective_id=0, has_side_effects=True
        ),
    )(sep_factor, coup_factor, anc_tiles)
    selected, variances = pl.pallas_call(
        last_kernel,
        out_shape=(
            jax.ShapeDtypeStruct((half, width), F32),
            jax.ShapeDtypeStruct((1, half), F32),
        ),
        in_specs=[smem, smem] + [hbm] * 4,
        out_specs=[hbm, vmem],
        scratch_shapes=[
            pltpu.VMEM((rows, rows), BF),
            pltpu.VMEM((rows, half), BF),
            pltpu.VMEM((rows, half), BF),
            pltpu.VMEM((half, rows), BF),
            pltpu.VMEM((half, width), F32),
            pltpu.SMEM((groups * slots,), jnp.int32),
            dma((4,)),
            dma((4,)),
            dma,
        ],
        compiler_params=pltpu.CompilerParams(vmem_limit_bytes=63 << 20),
    )(coup_list, slot_tiles, wide, wide_other, square, pool)
    return selected, variances.reshape(half)


def solution(mesh):
    placed = (P(("front", "panel"), None), P(("front", "panel"), None), P(), P(), P("front", None))
    return jax.shard_map(
        on_device,
        mesh=mesh,
        in_specs=placed,
        out_specs=(P(("front", "panel"), None), P(("front", "panel"))),
        check_vma=False,
    )
```

```python
import functools

import jax
import jax.numpy as jnp
from jax import lax
from jax.experimental import pallas as pl
from jax.experimental.pallas import tpu as pltpu
from jax.sharding import PartitionSpec as P

BF = jnp.bfloat16
F32 = jnp.float32
DIAG = 128
MESH = pl.DeviceIdType.MESH


def mm(a, b):
    return jnp.dot(a, b, preferred_element_type=F32)


def split(x):
    hi = x.astype(BF)
    return hi, (x - hi.astype(F32)).astype(BF)


def flip(index, mask):
    bit = 1
    while bit <= mask:
        if mask & bit:
            index = index + bit * (1 - 2 * ((index // bit) % 2))
        bit *= 2
    return index


def first_kernel(
    depth,
    sep_ref,
    coup_ref,
    anc_ref,
    wide_out,
    wide_other,
    square_out,
    pool_ref,
    inv_ref,
    wide_ref,
    square_ref,
    lmat,
    coup_all,
    xl,
    xd,
    panel_send,
    panel_recv,
    z_recv,
    x_recv,
    y_recv,
    first_recv,
    second_recv,
    share_recv,
    out_send,
    local_sem,
):
    me = lax.axis_index("panel")
    group = lax.axis_index("front")
    layer, spot = group // 4, group % 4
    half, n = sep_ref.shape[0], sep_ref.shape[1]
    slab = anc_ref.shape[0]
    part = slab // 2
    partner = (group, 1 - me)
    beside = (layer * 4 + flip(spot, 1), me)
    behind = (layer * 4 + flip(spot, 2), me)
    peers = [(flip(layer, k) * 4 + spot, me) for k in range(1, depth)]

    barrier = pltpu.get_barrier_semaphore()
    for device in [partner, beside, behind] + peers:
        pl.semaphore_signal(barrier, inc=1, device_id=device, device_id_type=MESH)
    pl.semaphore_wait(barrier, 2 + depth)

    def remote(source, target, send, recv, device):
        return pltpu.make_async_remote_copy(
            src_ref=source, dst_ref=target, send_sem=send, recv_sem=recv, device_id=device, device_id_type=MESH
        )

    def place(k, mask, low=0, size=part):
        owner = flip(layer, k) * 4 + flip(spot, mask)
        start = pl.multiple_of(owner * slab + me * part + low, part // 2)
        return pool_ref.at[pl.ds(start, size), :]

    def push(source, target, recv, device):
        remote(source, target, out_send, recv, device).start()

    def arrived(target, recv):
        remote(target, target, out_send, recv, partner).wait_recv()

    own = anc_ref.at[pl.ds(pl.multiple_of(me * part, part), part), :]

    def open_block(k):
        source = own if k == 0 else place(k, 0)
        if k > 0:
            arrived(source, z_recv.at[k])
        piece = part // 2
        for first in (True, False):
            for recv, device, low in (
                (x_recv, beside, piece if first else 0),
                (y_recv, behind, 0 if first else piece),
            ):
                push(
                    source.at[pl.ds(low, piece), :],
                    place(k, 0, low, piece),
                    recv.at[k if first else depth + k],
                    device,
                )
        if k > 0:
            push(source, source, share_recv, partner)

    def relay(k):
        piece = part // 2
        arrived(place(k, 1, piece, piece), x_recv.at[k])
        push(place(k, 1, piece, piece), place(k, 1, piece, piece), second_recv.at[k], behind)
        arrived(place(k, 2, 0, piece), y_recv.at[k])
        push(place(k, 2, 0, piece), place(k, 2, 0, piece), first_recv.at[k], beside)
        arrived(place(k, 1, 0, piece), x_recv.at[depth + k])
        arrived(place(k, 2, piece, piece), y_recv.at[depth + k])
        push(place(k, 1), place(k, 1), share_recv, partner)
        push(place(k, 2), place(k, 2), share_recv, partner)

    def finish(k):
        piece = part // 2
        arrived(place(k, 3, 0, piece), first_recv.at[k])
        arrived(place(k, 3, piece, piece), second_recv.at[k])
        push(place(k, 3), place(k, 3), share_recv, partner)

    def stage(k):
        if 2 <= k <= depth + 1:
            finish(k - 2)
        if 1 <= k <= depth:
            relay(k - 1)
        if k < depth:
            open_block(k)

    rows = coup_ref.shape[0]
    upper = pl.ds(pl.multiple_of(me * half, half), half)
    sep_copy = remote(sep_ref, lmat.at[upper, :], panel_send.at[0], panel_recv.at[0], partner)
    coup_copy = remote(coup_ref, coup_all.at[pl.ds(rows, rows), :], panel_send.at[1], panel_recv.at[1], partner)
    wide_copy = remote(wide_ref, wide_other, panel_send.at[2], panel_recv.at[2], partner)
    sep_keep = pltpu.make_async_copy(sep_ref, lmat.at[upper, :], local_sem.at[0])
    sep_copy.start()
    for k in range(1, depth):
        push(own, place(0, 0), z_recv.at[k], peers[k - 1])
        if k == 1:
            stage(0)
    coup_copy.start()
    sep_keep.start()
    coup_keep = pltpu.make_async_copy(coup_ref, coup_all.at[pl.ds(0, rows), :], local_sem.at[1])
    coup_keep.start()
    keep = pltpu.make_async_copy(
        anc_ref, pool_ref.at[pl.ds(pl.multiple_of(group * slab, slab), slab), :], local_sem.at[2]
    )
    keep.start()

    inv_ref[...] = jnp.zeros_like(inv_ref)
    xl[...] = jnp.zeros_like(xl)
    sep_keep.wait()
    remote(sep_ref, lmat.at[pl.ds(pl.multiple_of((1 - me) * half, half), half), :], panel_send.at[0], panel_recv.at[0], partner).wait_recv()

    blocks = n // DIAG
    row = lax.broadcasted_iota(jnp.int32, (DIAG, DIAG), 0)
    col = lax.broadcasted_iota(jnp.int32, (DIAG, DIAG), 1)
    eye = row == col
    for b in range(blocks):
        span = pl.ds(b * DIAG, DIAG)
        block = lmat[span, span].astype(F32)
        xd[b] = jnp.where(eye, 1.0 / jnp.where(eye, block, 1.0), 0.0)

    def level(step, carry):
        mask = (
            ((row >> (step + 1)) == (col >> (step + 1)))
            & (((row >> step) & 1) == 1)
            & (((col >> step) & 1) == 0)
        )
        for b in range(blocks):
            span = pl.ds(b * DIAG, DIAG)
            x = xd[b]
            hi, lo = split(x)
            below = jnp.where(mask, lmat[span, span].astype(F32), 0.0).astype(BF)
            y = mm(below, jnp.concatenate([hi, lo], axis=1))
            yhi, ylo = split(y[:, :DIAG] + y[:, DIAG:])
            t = mm(jnp.concatenate([hi, lo], axis=0), jnp.concatenate([yhi, ylo], axis=1))
            t = (t[:DIAG, :DIAG] + t[:DIAG, DIAG:]) + (t[DIAG:, :DIAG] + t[DIAG:, DIAG:])
            xd[b] = x - t
        return carry

    levels = DIAG.bit_length() - 1
    lax.fori_loop(0, levels // 2, level, 0)
    stage(1)
    lax.fori_loop(levels // 2, levels, level, 0)
    for b in range(blocks):
        span = pl.ds(b * DIAG, DIAG)
        inv_ref[span, span], xl[span, span] = split(xd[b])
    size = DIAG
    while size < n:
        for start in range(0, n, 2 * size):
            top, low = pl.ds(start, size), pl.ds(start + size, size)
            below = lmat[low, top]
            thi, tlo = split(mm(below, inv_ref[top, top]) + mm(below, xl[top, top]))
            t = mm(inv_ref[low, low], thi) + (mm(inv_ref[low, low], tlo) + mm(xl[low, low], thi))
            inv_ref[low, top], xl[low, top] = split(-t)
        size *= 2
    stage(2)

    chunk = min(512, rows)
    columns = pl.ds(pl.multiple_of(me * half, half), half)
    coup_keep.wait()
    coup_copy.wait_recv()

    @pl.loop(0, 2 * rows // chunk)
    def _(i):
        take = pl.ds(pl.multiple_of(i * chunk, chunk), chunk)
        wide_ref[take, :] = mm(coup_all[take, :], inv_ref[:, columns]).astype(BF)

    stage(3)
    wide_copy.start()
    wide_keep = pltpu.make_async_copy(wide_ref, wide_out, local_sem.at[3])
    wide_keep.start()
    strip = pool_ref.shape[0] - 4 * depth * slab
    blank = pltpu.make_async_copy(
        inv_ref.at[pl.ds(0, strip), pl.ds(n - DIAG, DIAG)], pool_ref.at[pl.ds(4 * depth * slab, strip), :], local_sem.at[4]
    )
    blank.start()

    @pl.loop(0, n // 256)
    def _(i):
        take = pl.ds(pl.multiple_of(i * 256, 256), 256)
        square_ref[:, take] = lax.dot_general(
            inv_ref[:, columns], inv_ref[:, take], (((0,), (0,)), ((), ())), preferred_element_type=F32
        )

    square_keep = pltpu.make_async_copy(square_ref, square_out, local_sem.at[5])
    square_keep.start()
    for k in range(4, depth + 2):
        stage(k)

    total = 4 * depth - 1
    shared = pool_ref.at[pl.ds(0, total * part), :]
    remote(shared, shared, out_send, share_recv, partner).wait_recv()
    sent = pool_ref.at[pl.ds(0, (2 * total) * part), :]
    remote(sent, sent, out_send, share_recv, partner).wait_send()
    for copy in (keep, wide_keep, blank, square_keep):
        copy.wait()
    sep_copy.wait_send()
    coup_copy.wait_send()
    wide_copy.wait()


def last_kernel(
    list_ref,
    slot_ref,
    wide_in,
    other_in,
    square_in,
    pool_ref,
    out_ref,
    var_ref,
    sigma,
    wide,
    wide_other,
    carried,
    out,
    place,
    tile_sem,
    load_sem,
    store_sem,
):
    me = lax.axis_index("panel")
    group = lax.axis_index("front")
    rows, half = wide.shape
    edge = pool_ref.shape[1]
    groups, slots = slot_ref.shape
    total = groups * slots
    strip_rows = rows * rows // (total * edge)
    strip_count = edge // strip_rows
    across = rows // edge
    chunks = tile_sem.shape[0]
    chunk = rows // chunks
    low, high = pl.ds(0, rows // 2), pl.ds(rows // 2, rows // 2)

    load_wide = pltpu.make_async_copy(wide_in, wide, load_sem.at[0])
    load_low = pltpu.make_async_copy(other_in.at[high, :], wide_other.at[low, :], load_sem.at[1])
    load_high = pltpu.make_async_copy(other_in.at[low, :], wide_other.at[high, :], load_sem.at[2])
    load_square = pltpu.make_async_copy(square_in, out, load_sem.at[3])
    load_wide.start()

    @pl.loop(0, groups)
    def _(g):
        for s in range(slots):
            place[slot_ref[g, s]] = g * slots + s

    def block(i):
        return list_ref[group, (i + me * (across // 2)) % across]

    def fetch(i):
        a = block(i)
        for j in range(across):
            b = block(j)
            live = (a >= 0) & (b >= 0)
            for q in range(strip_count):
                at = place[jnp.where(live, a * groups + b * strip_count + q, 0)]
                source = pl.multiple_of(jnp.where(live, at, total) * strip_rows, strip_rows)
                down = pl.multiple_of(i * edge + q * strip_rows, strip_rows)
                pltpu.make_async_copy(
                    pool_ref.at[pl.ds(source, strip_rows), :],
                    sigma.at[pl.ds(down, strip_rows), pl.ds(j * edge, edge)],
                    tile_sem.at[i // (across // chunks)],
                ).start()

    pl.loop(0, across)(fetch)
    load_low.start()
    load_high.start()
    load_square.start()
    load_wide.wait()

    @pl.loop(0, chunks)
    def _(i):
        take = pl.ds(pl.multiple_of(i * chunk, chunk), chunk)
        pltpu.make_async_copy(sigma.at[take, :], sigma.at[take, :], tile_sem.at[i]).wait()
        carried[:, take] = mm(sigma[take, :], wide[...]).T.astype(BF)

    load_low.wait()
    load_high.wait()
    load_square.wait()
    step = 256
    for source, base in ((wide, me), (wide_other, 1 - me)):
        for c in range(half // step):
            put = pl.ds(pl.multiple_of(base * half + c * step, step), step)
            out[:, put] += mm(carried[...], source[:, pl.ds(c * step, step)])
            pltpu.make_async_copy(out.at[:, put], out_ref.at[:, put], store_sem).start()
    block_out = out[:, pl.ds(pl.multiple_of(me * half, half), half)]
    row = lax.broadcasted_iota(jnp.int32, (half, half), 0)
    col = lax.broadcasted_iota(jnp.int32, (half, half), 1)
    var_ref[...] = jnp.sum(jnp.where(row == col, block_out, 0.0), axis=0, keepdims=True)
    pltpu.make_async_copy(out, out_ref, store_sem).wait()


def gather_kernel(
    depth,
    slot_ref,
    sep_ref,
    coup_ref,
    anc_ref,
    pool,
    wide,
    turned,
    out,
    strips,
    lmat,
    coup,
    inv_ref,
    xl,
    xd,
    panel_send,
    panel_recv,
    z_recv,
    x_recv,
    y_recv,
    first_recv,
    second_recv,
    share_recv,
    out_send,
    local_sem,
):
    me = lax.axis_index("panel")
    group = lax.axis_index("front")
    layer, spot = group // 4, group % 4
    half, n = sep_ref.shape
    groups, slots = slot_ref.shape
    edge = anc_ref.shape[1]
    side = edge // 2
    rows = coup_ref.shape[0]
    across = 2 * rows // edge
    mine = slots // 2
    body = mine * side
    part = body + across
    low_size = part // 32 * 16
    low_size = part - low_size if part % 32 else low_size
    partner = (group, 1 - me)
    beside = (layer * 4 + flip(spot, 1), me)
    behind = (layer * 4 + flip(spot, 2), me)
    peers = [(flip(layer, k) * 4 + spot, me) for k in range(1, depth)]

    strip_load = pltpu.make_async_copy(
        anc_ref.at[pl.ds(pl.multiple_of(me * mine * edge, mine * edge), mine * edge), :], strips, local_sem.at[0]
    )
    strip_load.start()
    upper = pl.ds(pl.multiple_of(me * half, half), half)
    sep_keep = pltpu.make_async_copy(sep_ref, lmat.at[upper, :], local_sem.at[1])
    sep_keep.start()
    coup_keep = pltpu.make_async_copy(coup_ref, coup, local_sem.at[2])
    coup_keep.start()

    barrier = pltpu.get_barrier_semaphore()
    for device in [partner, beside, behind] + peers:
        pl.semaphore_signal(barrier, inc=1, device_id=device, device_id_type=MESH)

    def remote(source, target, send, recv, device):
        return pltpu.make_async_remote_copy(
            src_ref=source, dst_ref=target, send_sem=send, recv_sem=recv, device_id=device, device_id_type=MESH
        )

    def place(k, mask, piece=None):
        owner = flip(layer, k) * 4 + flip(spot, mask)
        low, size = ((0, part), (0, low_size), (low_size, part - low_size))[0 if piece is None else piece + 1]
        start = pl.multiple_of((owner * 2 + me) * part + low, 16)
        return pool.at[pl.ds(start, size), :]

    def push(source, recv, device):
        remote(source, source, out_send, recv, device).start()

    def arrived(target, recv):
        remote(target, target, out_send, recv, partner).wait_recv()

    def open_block(k):
        if k > 0:
            arrived(place(k, 0), z_recv.at[k])
        for first in (True, False):
            for recv, device, piece in ((x_recv, beside, 1 if first else 0), (y_recv, behind, 0 if first else 1)):
                push(place(k, 0, piece), recv.at[k if first else depth + k], device)
        push(place(k, 0), share_recv, partner)

    def relay(k):
        arrived(place(k, 1, 1), x_recv.at[k])
        push(place(k, 1, 1), second_recv.at[k], behind)
        arrived(place(k, 2, 0), y_recv.at[k])
        push(place(k, 2, 0), first_recv.at[k], beside)

    def collect(k):
        arrived(place(k, 1, 0), x_recv.at[depth + k])
        arrived(place(k, 2, 1), y_recv.at[depth + k])
        push(place(k, 1), share_recv, partner)
        push(place(k, 2), share_recv, partner)

    def finish(k):
        arrived(place(k, 3, 0), first_recv.at[k])
        arrived(place(k, 3, 1), second_recv.at[k])
        push(place(k, 3), share_recv, partner)

    row = lax.broadcasted_iota(jnp.int32, (side, edge), 0)
    lane = lax.broadcasted_iota(jnp.int32, (side, edge), 1)
    left = lane < side
    column = jnp.where(left, lane, lane - side)
    left_flag = jnp.where(left, 1, 0)
    triangle = jnp.where(column >= row, 1, 0)
    list_row = lax.broadcasted_iota(jnp.int32, (across, edge), 0)
    mine_at = pl.multiple_of((group * 2 + me) * part, 16)
    strip_load.wait()
    extra = jnp.zeros((across, edge), F32)
    for s in range(mine):
        tile_id = slot_ref[group, me * mine + s]
        i, j = tile_id // across, tile_id % across
        tile = strips[s * edge : (s + 1) * edge, :].astype(F32)
        chosen = jnp.where(jnp.full((edge, edge), i - j) > 0, tile.T, tile)
        top, bottom = chosen[:side, :], chosen[side:, :]
        gap = jnp.full((side, edge), i - j)
        wanted = jnp.where(gap == 0, triangle, jnp.where(gap < 0, 1, 0))
        pool[pl.ds(mine_at + s * side, side), :] = jnp.where(left_flag == wanted, top, bottom).astype(BF)
        line = jnp.sum(jnp.where(column == row, jnp.where(left, bottom, top), 0.0), axis=0, keepdims=True)
        hit = jnp.where(jnp.full((across, edge), i - j) == 0, jnp.where(list_row == jnp.full((across, edge), i), 1, 0), 0)
        extra = extra + jnp.where(hit == 1, line, 0.0)
    pool[pl.ds(mine_at + body, across), :] = extra.astype(BF)

    pl.semaphore_wait(barrier, 2 + depth)
    sep_copy = remote(sep_ref, lmat.at[upper, :], panel_send.at[0], panel_recv.at[0], partner)
    sep_copy.start()
    for k in range(1, depth):
        push(place(0, 0), z_recv.at[k], peers[k - 1])
        if k == 1:
            open_block(0)

    inv_ref[...] = jnp.zeros_like(inv_ref)
    xl[...] = jnp.zeros_like(xl)
    wide[pl.ds(2 * rows, edge), :] = jnp.zeros((edge, n), BF)
    turned[:, pl.ds(2 * rows, edge)] = jnp.zeros((half, edge), BF)
    sep_keep.wait()
    other = pl.ds(pl.multiple_of((1 - me) * half, half), half)
    remote(sep_ref, lmat.at[other, :], panel_send.at[0], panel_recv.at[0], partner).wait_recv()

    blocks = n // DIAG
    row128 = lax.broadcasted_iota(jnp.int32, (DIAG, DIAG), 0)
    col128 = lax.broadcasted_iota(jnp.int32, (DIAG, DIAG), 1)
    eye = row128 == col128
    for b in range(blocks):
        span = pl.ds(b * DIAG, DIAG)
        block = lmat[span, span].astype(F32)
        xd[b] = jnp.where(eye, 1.0 / jnp.where(eye, block, 1.0), 0.0)

    def level(step, carry):
        mask = (
            ((row128 >> (step + 1)) == (col128 >> (step + 1)))
            & (((row128 >> step) & 1) == 1)
            & (((col128 >> step) & 1) == 0)
        )
        for b in range(blocks):
            span = pl.ds(b * DIAG, DIAG)
            x = xd[b]
            hi, lo = split(x)
            below = jnp.where(mask, lmat[span, span].astype(F32), 0.0).astype(BF)
            y = mm(below, jnp.concatenate([hi, lo], axis=1))
            yhi, ylo = split(y[:, :DIAG] + y[:, DIAG:])
            t = mm(jnp.concatenate([hi, lo], axis=0), jnp.concatenate([yhi, ylo], axis=1))
            t = (t[:DIAG, :DIAG] + t[:DIAG, DIAG:]) + (t[DIAG:, :DIAG] + t[DIAG:, DIAG:])
            xd[b] = x - t
        return carry

    def merge(size):
        for start in range(0, n, 2 * size):
            top, low = pl.ds(start, size), pl.ds(start + size, size)
            below = lmat[low, top]
            thi, tlo = split(mm(below, inv_ref[top, top]) + mm(below, xl[top, top]))
            t = mm(inv_ref[low, low], thi) + (mm(inv_ref[low, low], tlo) + mm(xl[low, low], thi))
            inv_ref[low, top], xl[low, top] = split(-t)

    levels = DIAG.bit_length() - 1
    lax.fori_loop(0, levels // 2, level, 0)
    relay(0)
    open_block(1)
    collect(0)
    lax.fori_loop(levels // 2, levels, level, 0)
    for b in range(blocks):
        span = pl.ds(b * DIAG, DIAG)
        inv_ref[span, span], xl[span, span] = split(xd[b])
    relay(1)
    merge(DIAG)
    open_block(2)
    finish(0)
    collect(1)
    size = 2 * DIAG
    while size < n:
        merge(size)
        size *= 2
    relay(2)
    coup_keep.wait()
    own_rows = pl.ds(pl.multiple_of(me * rows, rows), rows)
    step = 256
    for c in range(n // step):
        put = pl.ds(c * step, step)
        deep = pl.ds(c * step, n - c * step)
        wide[own_rows, put] = mm(coup[:, deep], inv_ref[deep, put]).astype(BF)
    open_block(3)
    finish(1)
    collect(2)
    wide_copy = remote(wide.at[own_rows, :], wide.at[own_rows, :], panel_send.at[1], panel_recv.at[1], partner)
    wide_copy.start()
    columns = pl.ds(pl.multiple_of(me * half, half), half)

    @pl.loop(0, n // step)
    def _(i):
        take = pl.ds(pl.multiple_of(i * step, step), step)
        out[:, take] = lax.dot_general(
            inv_ref[:, columns], inv_ref[:, take], (((0,), (0,)), ((), ())), preferred_element_type=F32
        )

    relay(3)
    finish(2)
    other_rows = pl.ds(pl.multiple_of((1 - me) * rows, rows), rows)
    remote(wide.at[other_rows, :], wide.at[other_rows, :], panel_send.at[1], panel_recv.at[1], partner).wait_recv()

    @pl.loop(0, across)
    def _(c):
        put = pl.ds(pl.multiple_of(c * edge, edge), edge)
        turned[:, put] = wide[put, columns].T

    collect(3)
    finish(3)
    total = 4 * depth
    shared = pool.at[pl.ds(0, total * part), :]
    remote(shared, shared, out_send, share_recv, partner).wait_recv()

    sent = pool.at[pl.ds(0, (2 * total - 1) * part), :]
    remote(sent, sent, out_send, share_recv, partner).wait_send()
    sep_copy.wait_send()
    wide_copy.wait_send()


def select_kernel(
    list_ref,
    slot_ref,
    pool,
    wide,
    flat,
    square,
    out_ref,
    var_ref,
    table,
    natural,
    turned,
    sigma,
    carried,
    out,
    load_sem,
    store_sem,
):
    me = lax.axis_index("panel")
    group = lax.axis_index("front")
    groups, slots = slot_ref.shape
    edge = pool.shape[1]
    side = edge // 2
    half, n = out.shape
    across = sigma.shape[0] // edge
    rows = sigma.shape[0] // 2
    mine = slots // 2
    body = mine * side
    part = body + across
    step = 256
    columns = pl.ds(pl.multiple_of(me * half, half), half)

    for c in range(across):
        at = across
        for a in range(across):
            at = jnp.where(list_ref[group, a] == c, a, at)
        source = pl.ds(pl.multiple_of(at * edge, edge), edge)
        put = pl.ds(c * edge, edge)
        pltpu.make_async_copy(flat.at[:, source], turned.at[:, put], load_sem.at[0]).start()
        pltpu.make_async_copy(wide.at[source, :], natural.at[put, :], load_sem.at[1]).start()

    @pl.loop(0, groups)
    def _(g):
        for s in range(slots):
            table[slot_ref[g, s]] = (g * 2 + s // mine) * part + (s % mine) * side

    row = lax.broadcasted_iota(jnp.int32, (side, edge), 0)
    lane = lax.broadcasted_iota(jnp.int32, (side, edge), 1)
    left = lane < side
    column = jnp.where(left, lane, lane - side)

    def packed(i, j):
        tile_id = i * across + j
        return pool[pl.ds(pl.multiple_of(table[tile_id], 16), side), :]

    def span_of(i):
        return pl.ds(pl.multiple_of(i * edge, edge), edge)

    extra = jnp.zeros((across, edge), F32)
    for g in range(2 * groups):
        extra = extra + pool[g * part + body : g * part + part, :].astype(F32)

    for i in range(across):
        p = packed(i, i).astype(F32)
        turn = jnp.concatenate([p, p], axis=0).T
        d = jnp.broadcast_to(extra[i : i + 1, :], (side, edge))
        keep, below, equal = column >= row, column < row, column == row
        top = jnp.where(left, jnp.where(keep, p, turn[:side]), jnp.where(below, p, jnp.where(equal, d, turn[:side])))
        bottom = jnp.where(left, jnp.where(below, p, jnp.where(equal, d, turn[side:])), jnp.where(keep, p, turn[side:]))
        sigma[i * edge : (i + 1) * edge, i * edge : (i + 1) * edge] = jnp.concatenate([top, bottom], axis=0).astype(BF)

    @pl.loop(0, across)
    def _(i):
        for d in range(1, across // 2 + 1):
            other = (i + d) % across
            a, b = jnp.minimum(i, other), jnp.maximum(i, other)
            p, q = packed(a, b), packed(b, a)
            sigma[span_of(a), span_of(b)] = jnp.concatenate([jnp.where(left, p, q), jnp.where(left, q, p)], axis=0)

    for i in range(0, across, 2):
        a, b = slice(i * edge, (i + 1) * edge), slice((i + 1) * edge, (i + 2) * edge)
        sigma[b, a] = sigma[a, b].astype(F32).T.astype(BF)

    pltpu.make_async_copy(turned, turned, load_sem.at[0]).wait()
    size = 2 * rows
    for c in range(size // step):
        put = slice(c * step, (c + 1) * step)
        end = (c + 1) * step
        value = mm(turned[:, :end], sigma[:end, put])
        if end < size:
            value = value + lax.dot_general(
                turned[:, end:], sigma[put, end:], (((1,), (1,)), ((), ())), preferred_element_type=F32
            )
        carried[:, put] = value.astype(BF)

    pltpu.make_async_copy(natural, natural, load_sem.at[1]).wait()
    for c in range(n // step):
        put = slice(c * step, (c + 1) * step)
        out[:, put] = square[:, put] + mm(carried[...], natural[:, put])
        pltpu.make_async_copy(out.at[:, put], out_ref.at[:, put], store_sem).start()
    block_out = out[:, columns]
    row_out = lax.broadcasted_iota(jnp.int32, (half, half), 0)
    col_out = lax.broadcasted_iota(jnp.int32, (half, half), 1)
    var_ref[...] = jnp.sum(jnp.where(row_out == col_out, block_out, 0.0), axis=0, keepdims=True)
    pltpu.make_async_copy(out, out_ref, store_sem).wait()


def on_device(sep_factor, coup_factor, coup_list, slot_tiles, anc_tiles):
    panels = lax.axis_size("panel")
    groups = lax.axis_size("front")
    half, width = sep_factor.shape
    edge = anc_tiles.shape[1]
    slots = slot_tiles.shape[1]
    strip_rows = anc_tiles.shape[0] // slots
    rows = coup_list.shape[1] * edge
    vmem = pl.BlockSpec(memory_space=pltpu.VMEM)
    smem = pl.BlockSpec(memory_space=pltpu.SMEM)
    hbm = pl.BlockSpec(memory_space=pltpu.HBM)
    depth = groups // 4
    dma = pltpu.SemaphoreType.DMA
    if strip_rows == edge:
        part = slots // 2 * (edge // 2) + rows // edge
        pool, wide, turned, square = pl.pallas_call(
            functools.partial(gather_kernel, depth),
            out_shape=(
                pltpu.VMEM((2 * groups * part, edge), BF),
                pltpu.VMEM((rows + edge, width), BF),
                pltpu.VMEM((half, rows + edge), BF),
                pltpu.VMEM((half, width), F32),
            ),
            in_specs=[smem] + [hbm] * 3,
            out_specs=[vmem] * 4,
            scratch_shapes=[
                pltpu.VMEM((slots // 2 * edge, edge), BF),
                pltpu.VMEM((width, width), BF),
                pltpu.VMEM((rows // 2, width), BF),
                pltpu.VMEM((width, width), BF),
                pltpu.VMEM((width, width), BF),
                pltpu.VMEM((width // DIAG, DIAG, DIAG), F32),
                dma((2,)),
                dma((2,)),
                dma((depth,)),
                dma((2 * depth,)),
                dma((2 * depth,)),
                dma((depth,)),
                dma((depth,)),
                dma,
                dma,
                dma((3,)),
            ],
            compiler_params=pltpu.CompilerParams(
                vmem_limit_bytes=50 << 20, collective_id=0, has_side_effects=True
            ),
        )(slot_tiles, sep_factor, coup_factor, anc_tiles)
        selected, variances = pl.pallas_call(
            select_kernel,
            out_shape=(
                jax.ShapeDtypeStruct((half, width), F32),
                jax.ShapeDtypeStruct((1, half), F32),
            ),
            in_specs=[smem, smem] + [vmem] * 4,
            out_specs=[hbm, vmem],
            scratch_shapes=[
                pltpu.SMEM((groups * slots,), jnp.int32),
                pltpu.VMEM((rows, width), BF),
                pltpu.VMEM((half, rows), BF),
                pltpu.VMEM((rows, rows), BF),
                pltpu.VMEM((half, rows), BF),
                pltpu.VMEM((half, width), F32),
                dma((2,)),
                dma,
            ],
            compiler_params=pltpu.CompilerParams(vmem_limit_bytes=36 << 20),
        )(coup_list, slot_tiles, pool, wide, turned, square)
        return selected, variances.reshape(half)
    wide, wide_other, square, pool = pl.pallas_call(
        functools.partial(first_kernel, depth),
        out_shape=(
            jax.ShapeDtypeStruct((rows, half), BF),
            jax.ShapeDtypeStruct((rows, half), BF),
            jax.ShapeDtypeStruct((half, width), F32),
            jax.ShapeDtypeStruct((groups * anc_tiles.shape[0] + strip_rows, edge), BF),
        ),
        in_specs=[hbm] * 3,
        out_specs=[hbm] * 4,
        scratch_shapes=[
            pltpu.VMEM((width, width), BF),
            pltpu.VMEM((rows, half), BF),
            pltpu.VMEM((half, width), F32),
            pltpu.VMEM((width, width), BF),
            pltpu.VMEM((rows, width), BF),
            pltpu.VMEM((width, width), BF),
            pltpu.VMEM((width // DIAG, DIAG, DIAG), F32),
            dma((3,)),
            dma((3,)),
            dma((depth,)),
            dma((2 * depth,)),
            dma((2 * depth,)),
            dma((depth,)),
            dma((depth,)),
            dma,
            dma,
            dma((6,)),
        ],
        compiler_params=pltpu.CompilerParams(
            vmem_limit_bytes=63 << 20, collective_id=0, has_side_effects=True
        ),
    )(sep_factor, coup_factor, anc_tiles)
    selected, variances = pl.pallas_call(
        last_kernel,
        out_shape=(
            jax.ShapeDtypeStruct((half, width), F32),
            jax.ShapeDtypeStruct((1, half), F32),
        ),
        in_specs=[smem, smem] + [hbm] * 4,
        out_specs=[hbm, vmem],
        scratch_shapes=[
            pltpu.VMEM((rows, rows), BF),
            pltpu.VMEM((rows, half), BF),
            pltpu.VMEM((rows, half), BF),
            pltpu.VMEM((half, rows), BF),
            pltpu.VMEM((half, width), F32),
            pltpu.SMEM((groups * slots,), jnp.int32),
            dma((4,)),
            dma((4,)),
            dma,
        ],
        compiler_params=pltpu.CompilerParams(vmem_limit_bytes=63 << 20),
    )(coup_list, slot_tiles, wide, wide_other, square, pool)
    return selected, variances.reshape(half)


def solution(mesh):
    placed = (P(("front", "panel"), None), P(("front", "panel"), None), P(), P(), P("front", None))
    return jax.shard_map(
        on_device,
        mesh=mesh,
        in_specs=placed,
        out_specs=(P(("front", "panel"), None), P(("front", "panel"))),
        check_vma=False,
    )
```
